256 devices in a mesh: dp: 32 (over z, y), tensor: 8 (over x, core).
Axes of the slice: x: 4, y: 4, z: 8, core: 2. Of those that a mesh axis runs over, the one named last changes fastest.
Arguments:
- hidden: bfloat16 [4096, 26624], P('dp', 'tensor'), may hold values from -6 to 6
- out_grad: bfloat16 [4096, 8192], P(('dp', 'tensor')), may hold values from -0.375 to 0.375
- master: float32 [8192, 26624], P('dp', 'tensor'), may hold values from -0.3125 to 0.3125
- first_moment: bfloat16 [8192, 26624], P('dp', 'tensor'), may hold values from -4 to 4
- second_moment: bfloat16 [8192, 26624], P('dp', 'tensor'), may hold values from 0.049804688 to 1
- row_counts: int32 [8], replicated, may hold values from 2816 to 3840, as said below
- step_count: int32 [1], replicated, may hold values from 1 to 11
Outputs:
- adam_update: float32 [8192, 26624], P('dp', 'tensor')
- weights_tp: bfloat16 [8192, 30720], P('dp', 'tensor')
The draws below stay inside these ranges and needn't reach their ends.
Inputs may be any that keep to these rules, and one draw needn't show every extreme that they name: Tensor index j takes row_counts[j] consecutive hidden units in order; they sum to 26624; offsets[j] differs from j * 3328 by at most 256; the largest count equals 3840.
All inputs are finite; a program needn't handle non-finite values.
Results may differ from the reference program's by a relative error of at most 0.0045.
Values may be sent and summed in bfloat16 or wider, within the bound.
No kernel may reach another device: no remote copies, remote signals or barrier semaphores. Data moves between devices by JAX's collectives and lax.ppermute only.
A program may use at most 192 MiB of HBM per device.

```python
import math
import jax
import jax.numpy as jnp
from jax import lax

D = 8192
FF_DEV = 3328
TOK_DEV = 128
DRIFT = 256
CAP = 3840
FF = 26624
TOKENS = 4096
N_DP = 32
N_TENSOR = 8


def draw_row_counts(key, part):
    base = jax.random.fold_in(key, 7)
    first_key, second_key = jax.random.split(base)
    moved = jax.random.randint(first_key, (N_TENSOR + 1,), -DRIFT, DRIFT + 1, dtype=jnp.int32)
    marked = jax.random.randint(second_key, (), 1, N_TENSOR - 1, dtype=jnp.int32)
    places = jnp.arange(N_TENSOR + 1, dtype=jnp.int32)
    moved = jnp.where(places == marked, -DRIFT, moved)
    moved = jnp.where(places == marked + 1, DRIFT, moved)
    moved = jnp.where((places == 0) | (places == N_TENSOR), 0, moved)
    return (FF_DEV + moved[1:] - moved[:-1]).astype(jnp.int32)


def raised(drawn, key, source, target, shards_of, factor):
    def block_of(position):
        return (jnp.arange(drawn.shape[position]) // (drawn.shape[position] // shards_of)).reshape((-1,) + (1,) * (drawn.ndim - 1 - position))

    near = jax.random.permutation(key, shards_of)[block_of(target)]
    far = (block_of(target) + shards_of // 2) % shards_of
    return jnp.where((block_of(source) == near) | (block_of(source) == far), factor * drawn, drawn)


def level_of(rng, shape, shards, least, high):
    loudness = 1.0
    for dim, blocks in shards:
        steps = jax.random.uniform(jax.random.fold_in(jax.random.fold_in(rng, 6), dim), (blocks,), jnp.float32, least / len(shards), high / len(shards))
        loudness = loudness * jnp.repeat(jnp.exp(steps), shape[dim] // blocks).reshape((-1,) + (1,) * (len(shape) - 1 - dim))
    return loudness


def noise(stream_key, extent, spread, most, pieces=(), held_as=jnp.bfloat16):
    result = jax.random.normal(stream_key, extent, jnp.float32) * spread
    if len(pieces) > 0:
        result = level_of(stream_key, extent, pieces, -0.22, 0.18) * result
    return jnp.clip(result, min=-most, max=most).astype(held_as)


def noise_with(rng, extent, scale, bound, cuts, heavy, kind=jnp.bfloat16):
    array = scale * jax.random.normal(rng, extent, jnp.float32)
    if cuts:
        array = array * level_of(rng, extent, cuts, -0.22, 0.18)
    return jnp.clip(raised(array, jax.random.fold_in(rng, 3), *heavy), -bound, bound).astype(kind)


def setup_inputs(seed: int = 0) -> dict:
    key_of = jax.random.split(jax.random.key(seed), 8)
    return {
        "hidden": noise(key_of[0], (TOKENS, FF), 1.0, 6.0, ((0, 32), (1, 8))),
        "out_grad": noise_with(key_of[1], (TOKENS, D), TOKENS ** -0.5, 0.375, ((0, 256),), (0, 1, 256, 6.0)),
        "master": noise(key_of[2], (D, FF), 0.02, 0.3125, ((0, 32), (1, 8)), jnp.float32),
        "first_moment": noise(key_of[3], (D, FF), 0.3, 4.0, ((0, 32), (1, 8))),
        "second_moment": jnp.clip(jnp.exp(math.log(1.0) - 2.9996462 * jax.random.uniform(key_of[4], (D, FF), jnp.float32) ** level_of(key_of[4], (D, FF), ((0, 32), (1, 8)), -0.2, 0.2)), 0.049804688, 1.0).astype(jnp.bfloat16),
        "row_counts": draw_row_counts(jax.random.fold_in(key_of[7], 71), 0),
        "step_count": jax.random.randint(key_of[6], (1,), 1, 12).astype(jnp.int32),
    }


beta_first = 0.9
beta_second = 0.95
epsilon = 1e-08
decay_rate = 0.1
learn_rate = 0.001

def adamw(gradient, master, first_moment, second_moment, steps_done):
    first_new = beta_first * first_moment + (1.0 - beta_first) * gradient
    second_new = beta_second * second_moment + (1.0 - beta_second) * gradient * gradient
    first_fix = 1.0 - jnp.power(beta_first, steps_done)
    second_fix = 1.0 - jnp.power(beta_second, steps_done)
    update = first_new / first_fix / (jnp.sqrt(second_new / second_fix) + epsilon) + decay_rate * master
    master_new = master - learn_rate * update
    return (master_new, update)

def reference(hidden, out_grad, master, first_moment, second_moment, row_counts, step_count):
    hidden_groups = hidden.reshape(N_DP, TOK_DEV, FF)
    grad_groups = out_grad.reshape(N_DP, TOK_DEV, D)

    def add_group(total, pair):
        activations, cotangent = pair
        partial_value = lax.dot_general(cotangent, activations, (((0,), (0,)), ((), ())), preferred_element_type=jnp.float32)
        rounded = lax.optimization_barrier(partial_value.astype(jnp.bfloat16)).astype(jnp.float32)
        return (total + rounded, None)
    gradient, unused = lax.scan(add_group, jnp.zeros((D, FF), jnp.float32), (hidden_groups, grad_groups))
    steps_done = step_count[0].astype(jnp.float32)
    master_new, update = adamw(gradient, master, first_moment.astype(jnp.float32), second_moment.astype(jnp.float32), steps_done)
    weights = master_new.astype(jnp.bfloat16)
    offsets = (jnp.cumsum(row_counts) - row_counts).astype(jnp.int32)
    slot_index = jnp.arange(CAP, dtype=jnp.int32)
    column_index = offsets[:, None] + slot_index[None, :]
    inside = slot_index[None, :] < row_counts[:, None]
    picked = jnp.take(weights, jnp.clip(column_index, 0, FF - 1).reshape(-1).astype(jnp.int32), axis=1)
    picked = picked.reshape(D, N_TENSOR, CAP)
    laid = jnp.where(inside[None], picked, jnp.zeros((), jnp.bfloat16)).reshape(D, N_TENSOR * CAP)
    return (update, laid)
```

```python
import jax
import jax.numpy as jnp
import numpy as np
from jax import lax
from jax.sharding import Mesh, PartitionSpec as P

DRIFT = 256
CAP = 3840
CHUNKS = ((0, 896), (2432, 3328), (896, 1664), (1664, 2432))

beta_first = 0.9
beta_second = 0.95
epsilon = 1e-08
decay_rate = 0.1
learn_rate = 0.001

TENSOR = ("x", "core")


def adamw(gradient, master, first_moment, second_moment, first_fix, second_fix):
    first_new = beta_first * first_moment + (1.0 - beta_first) * gradient
    second_new = beta_second * second_moment + (1.0 - beta_second) * gradient * gradient
    update = (
        first_new / first_fix / (jnp.sqrt(second_new / second_fix) + epsilon) + decay_rate * master
    )
    master_new = master - learn_rate * update
    return (master_new, update)


def per_device(hidden, out_grad, master, first_moment, second_moment, row_counts, step_count):
    width = hidden.shape[1]
    tensor_count = lax.axis_size(TENSOR)
    z_count = lax.axis_size("z")
    local_tokens = out_grad.shape[0]
    features = out_grad.shape[1] // z_count

    regrouped = lax.all_to_all(out_grad, "z", split_axis=1, concat_axis=0, tiled=True)
    spread = lax.all_gather(regrouped, TENSOR, axis=0, tiled=True)
    cotangent = spread.reshape(tensor_count, z_count, local_tokens, features)
    cotangent = cotangent.transpose(1, 0, 2, 3).reshape(-1, features)

    steps_done = step_count[0].astype(jnp.float32)
    first_fix = 1.0 - jnp.power(beta_first, steps_done)
    second_fix = 1.0 - jnp.power(beta_second, steps_done)

    gathered = [
        lax.all_gather(hidden[:, low:high], "z", axis=0, tiled=True) for low, high in CHUNKS
    ]
    updates = {}
    weights = {}
    for (low, high), acts in zip(CHUNKS, gathered):
        partial_value = lax.dot_general(
            cotangent, acts, (((0,), (0,)), ((), ())), preferred_element_type=jnp.float32
        ).astype(jnp.bfloat16)
        gradient = lax.psum_scatter(partial_value, "y", scatter_dimension=0, tiled=True)
        master_new, update = adamw(
            gradient.astype(jnp.float32),
            master[:, low:high],
            first_moment[:, low:high].astype(jnp.float32),
            second_moment[:, low:high].astype(jnp.float32),
            first_fix,
            second_fix,
        )
        updates[low] = update
        weights[low] = master_new.astype(jnp.bfloat16)

    order = sorted(updates)
    head = weights[order[0]][:, :DRIFT]
    tail = weights[order[-1]][:, -DRIFT:]
    ends = tensor_count - 1
    left = lax.ppermute(tail, TENSOR, [(i, i + 1) for i in range(ends)])
    right = lax.ppermute(head, TENSOR, [(i + 1, i) for i in range(ends)])

    position = lax.axis_index(TENSOR)
    places = jnp.arange(tensor_count, dtype=jnp.int32)
    first_slot = jnp.sum(jnp.where(places < position, row_counts, 0))
    length = jnp.sum(jnp.where(places == position, row_counts, 0))
    rows = master.shape[0]
    widened = jnp.concatenate(
        [left] + [weights[k] for k in order] + [right, jnp.zeros((rows, 2 * DRIFT), jnp.bfloat16)],
        axis=1,
    )
    start = first_slot - position * width + DRIFT
    window = lax.dynamic_slice_in_dim(widened, start, CAP, 1)
    slot_index = jnp.arange(CAP, dtype=jnp.int32)
    laid = jnp.where((slot_index < length)[None, :], window, jnp.zeros((), jnp.bfloat16))
    return (jnp.concatenate([updates[k] for k in order], axis=1), laid)


def solution(mesh):
    fine = Mesh(np.asarray(mesh.devices).reshape(8, 4, 4, 2), ("z", "y", "x", "core"))
    dp = ("z", "y")
    return jax.shard_map(
        per_device,
        mesh=fine,
        in_specs=(
            P(dp, TENSOR),
            P(dp + TENSOR, None),
            P(dp, TENSOR),
            P(dp, TENSOR),
            P(dp, TENSOR),
            P(),
            P(),
        ),
        out_specs=(P(dp, TENSOR), P(dp, TENSOR)),
        check_vma=False,
    )
```

```python
import jax
import jax.numpy as jnp
import numpy as np
from jax import lax
from jax.sharding import Mesh, PartitionSpec as P

DRIFT = 256
CAP = 3840
N_Z = 8
N_Y = 4
N_X = 4
LEFT = (0, 768)
RIGHT = (2560, 3328)
MIDDLE = ((768, 1664), (1664, 2560))

beta_first = 0.9
beta_second = 0.95
epsilon = 1e-08
decay_rate = 0.1
learn_rate = 0.001

TENSOR = ("x", "core")


def shift(value, axis, count, by):
    return lax.ppermute(value, axis, [(i, (i + by) % count) for i in range(count)])


def adamw(gradient, master, first_moment, second_moment, first_fix, second_fix):
    first_new = beta_first * first_moment + (1.0 - beta_first) * gradient
    second_new = beta_second * second_moment + (1.0 - beta_second) * gradient * gradient
    update = (
        first_new / first_fix / (jnp.sqrt(second_new / second_fix) + epsilon) + decay_rate * master
    )
    master_new = master - learn_rate * update
    return (master_new, update)


def ring_gather(block):
    z = lax.axis_index("z")
    rows, cols = block.shape
    half = rows // 2
    up = down = block
    pieces = [(block, 0)]
    for step in range(1, N_Z // 2):
        up = shift(up, "z", N_Z, 1)
        down = shift(down, "z", N_Z, -1)
        pieces += [(up, -step), (down, step)]
    last_up = shift(up[:half], "z", N_Z, 1)
    last_down = shift(down[half:], "z", N_Z, -1)
    full = jnp.zeros((rows * N_Z, cols), block.dtype)
    for piece, offset in pieces:
        full = lax.dynamic_update_slice_in_dim(full, piece, ((z + offset) % N_Z) * rows, 0)
    far = ((z + N_Z // 2) % N_Z) * rows
    full = lax.dynamic_update_slice_in_dim(full, last_up, far, 0)
    return lax.dynamic_update_slice_in_dim(full, last_down, far + half, 0)


def features_of(out_grad):
    x = lax.axis_index("x")
    core = lax.axis_index("core")
    tokens = out_grad.shape[0]
    mine = lax.all_to_all(out_grad, "z", split_axis=1, concat_axis=0, tiled=True)
    features = mine.shape[1]
    line = jnp.zeros((N_X,) + mine.shape, mine.dtype)
    for by in (0, 1, -1, 2):
        piece = shift(mine, "x", N_X, by) if by else mine
        line = lax.dynamic_update_slice_in_dim(line, piece[None], (x - by) % N_X, 0)
    other = shift(line, "core", 2, 1)
    first = jnp.where(core == 0, line, other)
    second = jnp.where(core == 0, other, line)
    both = jnp.stack([first, second], axis=1).reshape(N_X, 2, N_Z, tokens, features)
    return both.transpose(4, 2, 0, 1, 3).reshape(features, -1)


def partials(cotangent, acts):
    y = lax.axis_index("y")
    rows = cotangent.shape[0] // N_Y
    out = {}
    for by in (2, 1, 3, 0):
        mine = lax.dynamic_slice_in_dim(cotangent, ((y + by) % N_Y) * rows, rows, 0)
        out[by] = lax.dot_general(
            mine, acts, (((1,), (0,)), ((), ())), preferred_element_type=jnp.float32
        ).astype(jnp.bfloat16)
    return out


def ring_scatter(part):
    half = part[0].shape[0] // 2
    up = shift(part[2][:half], "y", N_Y, 1)
    down = shift(part[2][half:], "y", N_Y, -1)
    to_up = jnp.concatenate([part[1][:half] + up, part[1][half:]], axis=0)
    to_down = jnp.concatenate([part[3][:half], part[3][half:] + down], axis=0)
    from_below = shift(to_up, "y", N_Y, 1)
    from_above = shift(to_down, "y", N_Y, -1)
    wide = jnp.float32
    return part[0].astype(wide) + from_below.astype(wide) + from_above.astype(wide)


def per_device(hidden, out_grad, master, first_moment, second_moment, row_counts, step_count):
    width = hidden.shape[1]
    tensor_count = lax.axis_size(TENSOR)

    middle = lax.all_gather(hidden[:, MIDDLE[0][0] : MIDDLE[1][1]], "z", axis=0, tiled=True)
    acts = {
        LEFT: ring_gather(hidden[:, LEFT[0] : LEFT[1]]),
        RIGHT: ring_gather(hidden[:, RIGHT[0] : RIGHT[1]]),
    }
    for low, high in MIDDLE:
        acts[(low, high)] = middle[:, low - MIDDLE[0][0] : high - MIDDLE[0][0]]
    cotangent = features_of(out_grad)

    steps_done = step_count[0].astype(jnp.float32)
    first_fix = 1.0 - jnp.power(beta_first, steps_done)
    second_fix = 1.0 - jnp.power(beta_second, steps_done)

    updates = {}
    weights = {}
    for low, high in (LEFT, RIGHT) + MIDDLE:
        gradient = ring_scatter(partials(cotangent, acts[(low, high)]))
        master_new, update = adamw(
            gradient,
            master[:, low:high],
            first_moment[:, low:high].astype(jnp.float32),
            second_moment[:, low:high].astype(jnp.float32),
            first_fix,
            second_fix,
        )
        updates[low] = update
        weights[low] = master_new.astype(jnp.bfloat16)

    order = sorted(updates)
    head = weights[order[0]][:, :DRIFT]
    tail = weights[order[-1]][:, -DRIFT:]
    ends = tensor_count - 1
    left = lax.ppermute(tail, TENSOR, [(i, i + 1) for i in range(ends)])
    right = lax.ppermute(head, TENSOR, [(i + 1, i) for i in range(ends)])

    position = lax.axis_index(TENSOR)
    places = jnp.arange(tensor_count, dtype=jnp.int32)
    first_slot = jnp.sum(jnp.where(places < position, row_counts, 0))
    length = jnp.sum(jnp.where(places == position, row_counts, 0))
    rows = master.shape[0]
    widened = jnp.concatenate(
        [left] + [weights[k] for k in order] + [right, jnp.zeros((rows, 2 * DRIFT), jnp.bfloat16)],
        axis=1,
    )
    start = first_slot - position * width + DRIFT
    window = lax.dynamic_slice_in_dim(widened, start, CAP, 1)
    slot_index = jnp.arange(CAP, dtype=jnp.int32)
    laid = jnp.where((slot_index < length)[None, :], window, jnp.zeros((), jnp.bfloat16))
    return (jnp.concatenate([updates[k] for k in order], axis=1), laid)


def solution(mesh):
    fine = Mesh(np.asarray(mesh.devices).reshape(N_Z, N_Y, N_X, 2), ("z", "y", "x", "core"))
    dp = ("z", "y")
    return jax.shard_map(
        per_device,
        mesh=fine,
        in_specs=(
            P(dp, TENSOR),
            P(dp + TENSOR, None),
            P(dp, TENSOR),
            P(dp, TENSOR),
            P(dp, TENSOR),
            P(),
            P(),
        ),
        out_specs=(P(dp, TENSOR), P(dp, TENSOR)),
        check_vma=False,
    )
```

```python
import functools

import jax
import jax.numpy as jnp
import numpy as np
from jax import lax
from jax.experimental import pallas as pl
from jax.experimental.pallas import tpu as pltpu
from jax.sharding import Mesh, PartitionSpec as P

DRIFT = 256
CAP = 3840
N_Z = 8
N_Y = 4
N_X = 4
LEFT = 640
RIGHT = 2688

beta_first = 0.9
beta_second = 0.95
epsilon = 1e-08
decay_rate = 0.1
learn_rate = 0.001

TENSOR = ("x", "core")


def shift(value, axis, count, by):
    return lax.ppermute(value, axis, [(i, (i + by) % count) for i in range(count)])


def both_ways(up, down):
    return shift(up, "z", N_Z, 1), shift(down, "z", N_Z, -1)


def ring_gather(block, first, farther):
    up, down = first
    pieces = [(block, 0), (up, -1), (down, 1)]
    for step in range(2, N_Z // 2):
        up, down = both_ways(up, down)
        pieces += [(up, -step), (down, step)]
    last = shift(up if farther > 0 else down, "z", N_Z, farther)
    return pieces + [(last, N_Z // 2)]


def cotangent_of(mine, tokens):
    rows, features = mine.shape
    count = 2 * N_X
    y = lax.axis_index("y")
    copies = jnp.broadcast_to(mine[None], (count, rows, features))
    spread = lax.all_to_all(copies, TENSOR, split_axis=0, concat_axis=0, tiled=True)
    spread = spread.reshape(count, N_Z, tokens, features).transpose(1, 0, 2, 3)
    spread = spread.reshape(-1, features)
    size = features // N_Y
    cut = size // 2

    def taken(by, start):
        return lax.dynamic_slice_in_dim(spread, ((y + by) % N_Y) * size + start, cut, 1)

    order = ((2, 0), (1, cut), (2, cut), (3, 0), (1, 0), (3, cut), (0, 0), (0, cut))
    return jnp.concatenate([taken(*k) for k in order], axis=1)


def partials_body(offsets, z_ref, cot_ref, *refs):
    pieces = refs[: len(offsets)]
    outs = refs[len(offsets) : -1]
    acts_ref = refs[-1]
    z = z_ref[0]
    for piece, offset in zip(pieces, offsets):
        rows = piece.shape[0]
        group = lax.rem(z + (offset + N_Z), N_Z)
        acts_ref[pl.ds(pl.multiple_of(group * rows, rows), rows), :] = piece[...]
    low = 0
    for out in outs:
        size = out.shape[0]
        out[...] = lax.dot_general(
            cot_ref[:, low : low + size],
            acts_ref[...],
            (((0,), (0,)), ((), ())),
            preferred_element_type=jnp.float32,
        ).astype(out.dtype)
        low += size


def partials(z, cotangent, pieces, low, cols, tile):
    tokens, features = cotangent.shape
    rows = features // N_Y
    first = low // tile
    along = lambda i: (0, i)
    shifted = lambda i: (0, i + first)
    sizes = (rows, rows, rows, rows)
    kinds = (jnp.bfloat16, jnp.bfloat16, jnp.bfloat16, jnp.float32)
    body = functools.partial(partials_body, tuple(p[1] for p in pieces))
    return pl.pallas_call(
        body,
        grid=(cols // tile,),
        in_specs=[
            pl.BlockSpec(memory_space=pltpu.SMEM),
            pl.BlockSpec(cotangent.shape, lambda i: (0, 0)),
        ]
        + [pl.BlockSpec((p[0].shape[0], tile), shifted) for p in pieces],
        out_specs=[pl.BlockSpec((size, tile), along) for size in sizes],
        out_shape=[
            jax.ShapeDtypeStruct((size, cols), kind) for size, kind in zip(sizes, kinds)
        ],
        scratch_shapes=[pltpu.VMEM((tokens, tile), jnp.bfloat16)],
        compiler_params=pltpu.CompilerParams(vmem_limit_bytes=20 * 1024 * 1024),
        name="partials",
    )(z, cotangent, *[pltpu.with_memory_space_constraint(p[0], pltpu.HBM) for p in pieces])


def ring_scatter(part):
    up, down, near, own = part
    half = near.shape[0] // 2
    wide = jnp.float32
    below = shift(up, "y", N_Y, 1)
    above = shift(down, "y", N_Y, -1)
    on_up = (near[:half].astype(wide) + below[:half].astype(wide)).astype(jnp.bfloat16)
    on_down = (near[half:].astype(wide) + above[:half].astype(wide)).astype(jnp.bfloat16)
    far_up = shift(on_up, "y", N_Y, 1)
    far_down = shift(on_down, "y", N_Y, -1)
    direct = jnp.concatenate([above[half:], below[half:]], axis=0).astype(wide)
    through = jnp.concatenate([far_up, far_down], axis=0).astype(wide)
    return own + direct + through


def adamw(gradient, master, first_moment, second_moment, first_fix, second_fix):
    first_new = beta_first * first_moment + (1.0 - beta_first) * gradient
    second_new = beta_second * second_moment + (1.0 - beta_second) * gradient * gradient
    update = (
        first_new / first_fix / (jnp.sqrt(second_new / second_fix) + epsilon) + decay_rate * master
    )
    master_new = master - learn_rate * update
    return (master_new, update)


def per_device(hidden, out_grad, master, first_moment, second_moment, row_counts, step_count):
    width = hidden.shape[1]
    rows = master.shape[0]
    tensor_count = lax.axis_size(TENSOR)
    z = lax.axis_index("z").astype(jnp.int32).reshape(1)

    inner = hidden[:, LEFT:RIGHT]
    rim = jnp.concatenate([hidden[:, :LEFT], hidden[:, RIGHT:]], axis=1)
    rim_near = both_ways(rim, rim)
    inner_near = both_ways(inner, inner)
    mine = lax.all_to_all(out_grad, "z", split_axis=1, concat_axis=0, tiled=True)
    rim_pieces = ring_gather(rim, rim_near, 1)
    inner_pieces = ring_gather(inner, inner_near, -1)
    _, _, mine = lax.optimization_barrier((rim_near, inner_near, mine))
    cotangent = cotangent_of(mine, out_grad.shape[0])

    steps_done = step_count[0].astype(jnp.float32)
    first_fix = 1.0 - jnp.power(beta_first, steps_done)
    second_fix = 1.0 - jnp.power(beta_second, steps_done)

    rim_gradient = ring_scatter(
        partials(z, cotangent, rim_pieces, 0, rim.shape[1], rim.shape[1] // 2)
    )
    span = (RIGHT - LEFT) // 2
    first_gradient = ring_scatter(partials(z, cotangent, inner_pieces, 0, span, span // 2))
    second_gradient = ring_scatter(partials(z, cotangent, inner_pieces, span, span, span // 2))

    updates = {}
    weights = {}
    for low, high, gradient in (
        (0, LEFT, rim_gradient[:, :LEFT]),
        (RIGHT, width, rim_gradient[:, LEFT:]),
        (LEFT, LEFT + span, first_gradient),
        (LEFT + span, RIGHT, second_gradient),
    ):
        master_new, updates[low] = adamw(
            gradient,
            master[:, low:high],
            first_moment[:, low:high].astype(jnp.float32),
            second_moment[:, low:high].astype(jnp.float32),
            first_fix,
            second_fix,
        )
        weights[low] = master_new.astype(jnp.bfloat16)
    head = weights[0][:, :DRIFT]
    tail = weights[RIGHT][:, -DRIFT:]
    last = tensor_count - 1
    left = lax.ppermute(tail, TENSOR, [(i, i + 1) for i in range(last)])
    right = lax.ppermute(head, TENSOR, [(i + 1, i) for i in range(last)])
    blank = jnp.zeros((rows, 2 * DRIFT), jnp.bfloat16)
    order = sorted(weights)
    widened = jnp.concatenate(
        [left] + [weights[k] for k in order] + [right, blank], axis=1
    )
    update = jnp.concatenate([updates[k] for k in order], axis=1)

    position = lax.axis_index(TENSOR)
    places = jnp.arange(tensor_count, dtype=jnp.int32)
    first_slot = jnp.sum(jnp.where(places < position, row_counts, 0))
    length = jnp.sum(jnp.where(places == position, row_counts, 0))
    start = first_slot - position * width + DRIFT
    window = lax.dynamic_slice_in_dim(widened, start, CAP, 1)
    slot_index = jnp.arange(CAP, dtype=jnp.int32)
    laid = jnp.where((slot_index < length)[None, :], window, jnp.zeros((), jnp.bfloat16))
    return (update, laid)


def solution(mesh):
    fine = Mesh(np.asarray(mesh.devices).reshape(N_Z, N_Y, N_X, 2), ("z", "y", "x", "core"))
    dp = ("z", "y")
    return jax.shard_map(
        per_device,
        mesh=fine,
        in_specs=(
            P(dp, TENSOR),
            P(dp + TENSOR, None),
            P(dp, TENSOR),
            P(dp, TENSOR),
            P(dp, TENSOR),
            P(),
            P(),
        ),
        out_specs=(P(dp, TENSOR), P(dp, TENSOR)),
        check_vma=False,
    )
```

```python
import functools

import jax
import jax.numpy as jnp
import numpy as np
from jax import lax
from jax.experimental import pallas as pl
from jax.experimental.pallas import tpu as pltpu
from jax.sharding import Mesh, PartitionSpec as P

DRIFT = 256
CAP = 3840
N_Z = 8
N_Y = 4
N_X = 4
LEFT = 640
MIDDLE = 1664
RIGHT = 2688
SPAN = 512

beta_first = 0.9
beta_second = 0.95
epsilon = 1e-08
decay_rate = 0.1
learn_rate = 0.001

TENSOR = ("x", "core")


def shift(value, axis, count, by):
    return lax.ppermute(value, axis, [(i, (i + by) % count) for i in range(count)])


def both_ways(up, down):
    return shift(up, "z", N_Z, 1), shift(down, "z", N_Z, -1)


def ring_gather(block, first, farther):
    up, down = first
    pieces = [(block, 0), (up, -1), (down, 1)]
    for step in range(2, N_Z // 2):
        up, down = both_ways(up, down)
        pieces += [(up, -step), (down, step)]
    last = shift(up if farther > 0 else down, "z", N_Z, farther)
    return pieces + [(last, N_Z // 2)]


def cotangent_of(mine, tokens):
    rows, features = mine.shape
    count = 2 * N_X
    y = lax.axis_index("y")
    copies = jnp.broadcast_to(mine[None], (count, rows, features))
    spread = lax.all_to_all(copies, TENSOR, split_axis=0, concat_axis=0, tiled=True)
    spread = spread.reshape(count, N_Z, tokens, features).transpose(1, 0, 2, 3)
    spread = spread.reshape(-1, features)
    size = features // N_Y
    cut = size // 2

    def taken(by, start):
        return lax.dynamic_slice_in_dim(spread, ((y + by) % N_Y) * size + start, cut, 1)

    order = ((2, 0), (1, cut), (2, cut), (3, 0), (1, 0), (3, cut), (0, 0), (0, cut))
    return jnp.concatenate([taken(*k) for k in order], axis=1)


def partials_body(offsets, z_ref, cot_ref, *refs):
    pieces = refs[: len(offsets)]
    outs = refs[len(offsets) : -1]
    acts_ref = refs[-1]
    z = z_ref[0]
    for piece, offset in zip(pieces, offsets):
        rows = piece.shape[0]
        group = lax.rem(z + (offset + N_Z), N_Z)
        acts_ref[pl.ds(pl.multiple_of(group * rows, rows), rows), :] = piece[...]
    low = 0
    for out in outs:
        size = out.shape[0]
        out[...] = lax.dot_general(
            cot_ref[:, low : low + size],
            acts_ref[...],
            (((0,), (0,)), ((), ())),
            preferred_element_type=jnp.float32,
        ).astype(out.dtype)
        low += size


def half_partials(z, cotangent, pieces, low, cols, tile, which, kinds):
    tokens, features = cotangent.shape
    rows = features // N_Y
    first = low // tile
    along = lambda i: (0, i)
    shifted = lambda i: (0, i + first)
    body = functools.partial(partials_body, tuple(p[1] for p in pieces))
    return pl.pallas_call(
        body,
        grid=(cols // tile,),
        in_specs=[
            pl.BlockSpec(memory_space=pltpu.SMEM),
            pl.BlockSpec((tokens, 2 * rows), lambda i: (0, which)),
        ]
        + [pl.BlockSpec((p[0].shape[0], tile), shifted) for p in pieces],
        out_specs=[pl.BlockSpec((rows, tile), along) for _ in kinds],
        out_shape=[jax.ShapeDtypeStruct((rows, cols), kind) for kind in kinds],
        scratch_shapes=[pltpu.VMEM((tokens, tile), jnp.bfloat16)],
        compiler_params=pltpu.CompilerParams(vmem_limit_bytes=16 * 1024 * 1024),
        name="partials",
    )(z, cotangent, *[pltpu.with_memory_space_constraint(p[0], pltpu.HBM) for p in pieces])


def partials(z, cotangent, pieces, low, cols, tile):
    take = functools.partial(half_partials, z, cotangent, pieces, low, cols, tile)
    return *take(0, (jnp.bfloat16, jnp.bfloat16)), *take(1, (jnp.bfloat16, jnp.float32))


def ring_scatter(part):
    up, down, near, own = part
    half = near.shape[0] // 2
    wide = jnp.float32
    below = shift(up, "y", N_Y, 1)
    above = shift(down, "y", N_Y, -1)
    on_up = (near[:half].astype(wide) + below[:half].astype(wide)).astype(jnp.bfloat16)
    on_down = (near[half:].astype(wide) + above[:half].astype(wide)).astype(jnp.bfloat16)
    far_up = shift(on_up, "y", N_Y, 1)
    far_down = shift(on_down, "y", N_Y, -1)
    direct = jnp.concatenate([above[half:], below[half:]], axis=0).astype(wide)
    through = jnp.concatenate([far_up, far_down], axis=0).astype(wide)
    return own + direct + through


def adamw(gradient, master, first_moment, second_moment, first_fix, second_fix):
    first_new = beta_first * first_moment + (1.0 - beta_first) * gradient
    second_new = beta_second * second_moment + (1.0 - beta_second) * gradient * gradient
    update = (
        first_new / first_fix / (jnp.sqrt(second_new / second_fix) + epsilon) + decay_rate * master
    )
    master_new = master - learn_rate * update
    return (master_new, update)


def per_device(hidden, out_grad, master, first_moment, second_moment, row_counts, step_count):
    width = hidden.shape[1]
    rows = master.shape[0]
    tensor_count = lax.axis_size(TENSOR)
    z = lax.axis_index("z").astype(jnp.int32).reshape(1)

    inner = hidden[:, LEFT:RIGHT]
    rim = jnp.concatenate([hidden[:, :LEFT], hidden[:, RIGHT:]], axis=1)
    rim_near = both_ways(rim, rim)
    inner_near = both_ways(inner, inner)
    mine = lax.all_to_all(out_grad, "z", split_axis=1, concat_axis=0, tiled=True)
    rim_pieces = ring_gather(rim, rim_near, 1)
    inner_pieces = ring_gather(inner, inner_near, -1)
    _, _, mine = lax.optimization_barrier((rim_near, inner_near, mine))
    cotangent = cotangent_of(mine, out_grad.shape[0])

    steps_done = step_count[0].astype(jnp.float32)
    first_fix = 1.0 - jnp.power(beta_first, steps_done)
    second_fix = 1.0 - jnp.power(beta_second, steps_done)

    rim_gradient = ring_scatter(
        partials(z, cotangent, rim_pieces, 0, rim.shape[1], rim.shape[1] // 2)
    )
    span = MIDDLE - LEFT
    rest = RIGHT - MIDDLE
    first_gradient = ring_scatter(partials(z, cotangent, inner_pieces, 0, span, SPAN))
    second_gradient = ring_scatter(partials(z, cotangent, inner_pieces, span, rest, SPAN))

    updates = {}
    weights = {}
    for low, high, gradient in (
        (0, LEFT, rim_gradient[:, :LEFT]),
        (RIGHT, width, rim_gradient[:, LEFT:]),
        (LEFT, LEFT + span, first_gradient),
        (LEFT + span, RIGHT, second_gradient),
    ):
        master_new, updates[low] = adamw(
            gradient,
            master[:, low:high],
            first_moment[:, low:high].astype(jnp.float32),
            second_moment[:, low:high].astype(jnp.float32),
            first_fix,
            second_fix,
        )
        weights[low] = master_new.astype(jnp.bfloat16)
    head = weights[0][:, :DRIFT]
    tail = weights[RIGHT][:, -DRIFT:]
    last = tensor_count - 1
    left = lax.ppermute(tail, TENSOR, [(i, i + 1) for i in range(last)])
    right = lax.ppermute(head, TENSOR, [(i + 1, i) for i in range(last)])
    widened = jnp.zeros((rows, width + 4 * DRIFT), jnp.bfloat16)
    widened = lax.dynamic_update_slice(widened, left, (0, 0))
    widened = lax.dynamic_update_slice(widened, right, (0, width + DRIFT))
    update = jnp.zeros((rows, width), jnp.float32)
    for low in weights:
        update = lax.dynamic_update_slice(update, updates[low], (0, low))
        widened = lax.dynamic_update_slice(widened, weights[low], (0, low + DRIFT))

    position = lax.axis_index(TENSOR)
    places = jnp.arange(tensor_count, dtype=jnp.int32)
    first_slot = jnp.sum(jnp.where(places < position, row_counts, 0))
    length = jnp.sum(jnp.where(places == position, row_counts, 0))
    start = first_slot - position * width + DRIFT
    window = lax.dynamic_slice_in_dim(widened, start, CAP, 1)
    slot_index = jnp.arange(CAP, dtype=jnp.int32)
    laid = jnp.where((slot_index < length)[None, :], window, jnp.zeros((), jnp.bfloat16))
    return (update, laid)


def solution(mesh):
    fine = Mesh(np.asarray(mesh.devices).reshape(N_Z, N_Y, N_X, 2), ("z", "y", "x", "core"))
    dp = ("z", "y")
    return jax.shard_map(
        per_device,
        mesh=fine,
        in_specs=(
            P(dp, TENSOR),
            P(dp + TENSOR, None),
            P(dp, TENSOR),
            P(dp, TENSOR),
            P(dp, TENSOR),
            P(),
            P(),
        ),
        out_specs=(P(dp, TENSOR), P(dp, TENSOR)),
        check_vma=False,
    )
```

```python
import functools

import jax
import jax.numpy as jnp
import numpy as np
from jax import lax
from jax.experimental import pallas as pl
from jax.experimental.pallas import tpu as pltpu
from jax.sharding import Mesh, PartitionSpec as P

DRIFT = 256
CAP = 3840
N_Z = 8
N_Y = 4
N_X = 4
LEFT = 640
MIDDLE = 1664
RIGHT = 2688
SPAN = 512

beta_first = 0.9
beta_second = 0.95
epsilon = 1e-08
decay_rate = 0.1
learn_rate = 0.001

TENSOR = ("x", "core")


def shift(value, axis, count, by):
    return lax.ppermute(value, axis, [(i, (i + by) % count) for i in range(count)])


def both_ways(up, down):
    return shift(up, "z", N_Z, 1), shift(down, "z", N_Z, -1)


def ring_gather(block, first, farther):
    up, down = first
    pieces = [(block, 0), (up, -1), (down, 1)]
    for step in range(2, N_Z // 2):
        up, down = both_ways(up, down)
        pieces += [(up, -step), (down, step)]
    last = shift(up if farther > 0 else down, "z", N_Z, farther)
    return pieces + [(last, N_Z // 2)]


def cotangent_of(mine, tokens):
    rows, features = mine.shape
    count = 2 * N_X
    y = lax.axis_index("y")
    copies = jnp.broadcast_to(mine[None], (count, rows, features))
    spread = lax.all_to_all(copies, TENSOR, split_axis=0, concat_axis=0, tiled=True)
    spread = spread.reshape(count, N_Z, tokens, features).transpose(1, 0, 2, 3)
    spread = spread.reshape(-1, features)
    size = features // N_Y
    cut = size // 2

    def taken(by, start):
        return lax.dynamic_slice_in_dim(spread, ((y + by) % N_Y) * size + start, cut, 1)

    order = ((2, 0), (1, cut), (2, cut), (3, 0), (1, 0), (3, cut), (0, 0), (0, cut))
    return jnp.concatenate([taken(*k) for k in order], axis=1)


def partials_body(offsets, z_ref, cot_ref, *refs):
    pieces = refs[: len(offsets)]
    outs = refs[len(offsets) : -1]
    acts_ref = refs[-1]
    z = z_ref[0]
    for piece, offset in zip(pieces, offsets):
        rows = piece.shape[0]
        group = lax.rem(z + (offset + N_Z), N_Z)
        acts_ref[pl.ds(pl.multiple_of(group * rows, rows), rows), :] = piece[...]
    low = 0
    for out in outs:
        size = out.shape[0]
        out[...] = lax.dot_general(
            cot_ref[:, low : low + size],
            acts_ref[...],
            (((0,), (0,)), ((), ())),
            preferred_element_type=jnp.float32,
        ).astype(out.dtype)
        low += size


def half_partials(z, cotangent, pieces, low, cols, tile, which, kinds):
    tokens, features = cotangent.shape
    rows = features // N_Y
    first = low // tile
    along = lambda i: (0, i)
    shifted = lambda i: (0, i + first)
    body = functools.partial(partials_body, tuple(p[1] for p in pieces))
    return pl.pallas_call(
        body,
        grid=(cols // tile,),
        in_specs=[
            pl.BlockSpec(memory_space=pltpu.SMEM),
            pl.BlockSpec((tokens, 2 * rows), lambda i: (0, which)),
        ]
        + [pl.BlockSpec((p[0].shape[0], tile), shifted) for p in pieces],
        out_specs=[pl.BlockSpec((rows, tile), along) for _ in kinds],
        out_shape=[jax.ShapeDtypeStruct((rows, cols), kind) for kind in kinds],
        scratch_shapes=[pltpu.VMEM((tokens, tile), jnp.bfloat16)],
        compiler_params=pltpu.CompilerParams(vmem_limit_bytes=16 * 1024 * 1024),
        name="partials",
    )(z, cotangent, *[pltpu.with_memory_space_constraint(p[0], pltpu.HBM) for p in pieces])


def partials(z, cotangent, pieces, low, cols, tile):
    take = functools.partial(half_partials, z, cotangent, pieces, low, cols, tile)
    return *take(0, (jnp.bfloat16, jnp.bfloat16)), *take(1, (jnp.bfloat16, jnp.float32))


def ring_scatter(part):
    up, down, near, own = part
    half = near.shape[0] // 2
    wide = jnp.float32
    below = shift(up, "y", N_Y, 1)
    above = shift(down, "y", N_Y, -1)
    on_up = (near[:half].astype(wide) + below[:half].astype(wide)).astype(jnp.bfloat16)
    on_down = (near[half:].astype(wide) + above[:half].astype(wide)).astype(jnp.bfloat16)
    far_up = shift(on_up, "y", N_Y, 1)
    far_down = shift(on_down, "y", N_Y, -1)
    direct = jnp.concatenate([above[half:], below[half:]], axis=0).astype(wide)
    through = jnp.concatenate([far_up, far_down], axis=0).astype(wide)
    return own + direct + through


def adamw(gradient, master, first_moment, second_moment, first_fix, second_fix):
    first_new = beta_first * first_moment + (1.0 - beta_first) * gradient
    second_new = beta_second * second_moment + (1.0 - beta_second) * gradient * gradient
    update = (
        first_new * first_fix / (jnp.sqrt(second_new * second_fix) + epsilon) + decay_rate * master
    )
    master_new = master - learn_rate * update
    return (master_new, update)


def per_device(hidden, out_grad, master, first_moment, second_moment, row_counts, step_count):
    width = hidden.shape[1]
    rows = master.shape[0]
    tensor_count = lax.axis_size(TENSOR)
    z = lax.axis_index("z").astype(jnp.int32).reshape(1)

    inner = hidden[:, LEFT:RIGHT]
    rim = jnp.concatenate([hidden[:, :LEFT], hidden[:, RIGHT:]], axis=1)
    rim_near = both_ways(rim, rim)
    inner_near = both_ways(inner, inner)
    mine = lax.all_to_all(out_grad, "z", split_axis=1, concat_axis=0, tiled=True)
    rim_pieces = ring_gather(rim, rim_near, 1)
    inner_pieces = ring_gather(inner, inner_near, -1)
    _, _, mine = lax.optimization_barrier((rim_near, inner_near, mine))
    cotangent = cotangent_of(mine, out_grad.shape[0])

    steps_done = step_count[0].astype(jnp.float32)
    first_fix = 1.0 / (1.0 - jnp.power(beta_first, steps_done))
    second_fix = 1.0 / (1.0 - jnp.power(beta_second, steps_done))

    rim_gradient = ring_scatter(
        partials(z, cotangent, rim_pieces, 0, rim.shape[1], rim.shape[1] // 2)
    )
    span = MIDDLE - LEFT
    rest = RIGHT - MIDDLE
    first_gradient = ring_scatter(partials(z, cotangent, inner_pieces, 0, span, SPAN))
    second_gradient = ring_scatter(partials(z, cotangent, inner_pieces, span, rest, SPAN))

    updates = {}
    weights = {}
    for low, high, gradient in (
        (0, LEFT, rim_gradient[:, :LEFT]),
        (RIGHT, width, rim_gradient[:, LEFT:]),
        (LEFT, LEFT + span, first_gradient),
        (LEFT + span, RIGHT, second_gradient),
    ):
        master_new, updates[low] = adamw(
            gradient,
            master[:, low:high],
            first_moment[:, low:high].astype(jnp.float32),
            second_moment[:, low:high].astype(jnp.float32),
            first_fix,
            second_fix,
        )
        weights[low] = master_new.astype(jnp.bfloat16)
    head = weights[0][:, :DRIFT]
    tail = weights[RIGHT][:, -DRIFT:]
    last = tensor_count - 1
    left = lax.ppermute(tail, TENSOR, [(i, i + 1) for i in range(last)])
    right = lax.ppermute(head, TENSOR, [(i + 1, i) for i in range(last)])
    widened = jnp.zeros((rows, width + 4 * DRIFT), jnp.bfloat16)
    widened = lax.dynamic_update_slice(widened, left, (0, 0))
    widened = lax.dynamic_update_slice(widened, right, (0, width + DRIFT))
    update = jnp.zeros((rows, width), jnp.float32)
    for low in weights:
        update = lax.dynamic_update_slice(update, updates[low], (0, low))
        widened = lax.dynamic_update_slice(widened, weights[low], (0, low + DRIFT))

    position = lax.axis_index(TENSOR)
    places = jnp.arange(tensor_count, dtype=jnp.int32)
    first_slot = jnp.sum(jnp.where(places < position, row_counts, 0))
    length = jnp.sum(jnp.where(places == position, row_counts, 0))
    start = first_slot - position * width + DRIFT
    window = lax.dynamic_slice_in_dim(widened, start, CAP, 1)
    slot_index = jnp.arange(CAP, dtype=jnp.int32)
    laid = jnp.where((slot_index < length)[None, :], window, jnp.zeros((), jnp.bfloat16))
    return (update, laid)


def solution(mesh):
    fine = Mesh(np.asarray(mesh.devices).reshape(N_Z, N_Y, N_X, 2), ("z", "y", "x", "core"))
    dp = ("z", "y")
    return jax.shard_map(
        per_device,
        mesh=fine,
        in_specs=(
            P(dp, TENSOR),
            P(dp + TENSOR, None),
            P(dp, TENSOR),
            P(dp, TENSOR),
            P(dp, TENSOR),
            P(),
            P(),
        ),
        out_specs=(P(dp, TENSOR), P(dp, TENSOR)),
        check_vma=False,
    )
```
